512 devices in a mesh: seq: 16 (over z, core), chan: 32 (over x, y).
Axes of the slice: x: 4, y: 8, z: 8, core: 2. Of those that a mesh axis runs over, the one named last changes fastest.
Arguments:
- query_proj: bfloat16 [4096, 4096], P('seq', 'chan'), may hold values from -6 to 6
- key_proj: bfloat16 [4096, 4096], P('seq', 'chan'), may hold values from -6 to 6
- value_proj: bfloat16 [4096, 4096], P('seq', 'chan'), may hold values from -6 to 6
- filter_in: float32 [32, 64], replicated, may hold values from -16 to 16
- filter_bias: float32 [64], replicated, may hold values from -3.140625 to 3.140625
- filter_out: float32 [64, 4096], P(None, 'chan'), may hold values from -0.75 to 0.75
- decay_level: float32 [4096], P('chan'), may hold values from 0 to 1
- skip_gain: float32 [4096], P('chan'), may hold values from -4 to 4
- out_weight: bfloat16 [4096, 4096], P(None, 'chan'), may hold values from -0.1875 to 0.1875
Outputs:
- mixed: bfloat16 [4096, 4096], P('seq', 'chan')
The draws below stay inside these ranges and needn't reach their ends.
All inputs are finite; a program needn't handle non-finite values.
Results may differ from the reference program's by a relative error of at most 0.019.
Values may be sent and summed in bfloat16 or wider, within the bound.
No kernel may reach another device: no remote copies, remote signals or barrier semaphores. Data moves between devices by JAX's collectives and lax.ppermute only.
A program may use at most 64 MiB of HBM per device.

```python
import math
import jax
import jax.numpy as jnp
from jax import lax

CH_DEV = 128
CH = 4096
DOUT = 4096
TOK_DEV = 256
TOKENS = 4096
POS = 32
ORDER = 64
N_SEQ = 16
N_CHAN = 32


def with_spikes(array, own_key, source, target, shards_of, factor):
    def block_of(dim):
        return (jnp.arange(array.shape[dim]) // (array.shape[dim] // shards_of)).reshape((-1,) + (1,) * (array.ndim - 1 - dim))

    first = jax.random.permutation(own_key, shards_of)[block_of(target)]
    second = (block_of(target) + shards_of // 2) % shards_of
    return jnp.where((block_of(source) == first) | (block_of(source) == second), factor * array, array)


def block_levels(rng, extent, pieces, smallest, largest):
    loudness, own = 1.0, jax.random.fold_in(rng, 6)
    for axis_at, parts in pieces:
        steps = jnp.exp(jax.random.uniform(jax.random.fold_in(own, axis_at), (parts,), jnp.float32, smallest / len(pieces), largest / len(pieces)))
        loudness = loudness * jnp.repeat(steps, extent[axis_at] // parts).reshape([-1 if axis == axis_at else 1 for axis in range(len(extent))])
    return loudness


def gaussian(stream_key, extent, scale, bound, split=(), kind=jnp.bfloat16):
    array = jax.random.normal(stream_key, extent, jnp.float32) * scale
    if len(split) > 0:
        array = block_levels(stream_key, extent, split, -0.22, 0.18) * array
    return jnp.clip(array, min=-bound, max=bound).astype(kind)


def bell_draw_with(rng, dims, deviation, reach, shards, heavy, held_as=jnp.bfloat16):
    result = deviation * jax.random.normal(rng, dims, jnp.float32)
    if shards:
        result = result * block_levels(rng, dims, shards, -0.22, 0.18)
    return jnp.clip(with_spikes(result, jax.random.fold_in(rng, 3), *heavy), -reach, reach).astype(held_as)


def setup_inputs(seed: int = 0) -> dict:
    seeds = jax.random.split(jax.random.key(seed), 10)
    return {
        "query_proj": gaussian(seeds[0], (TOKENS, CH), 1.0, 6.0, ((0, 16), (1, 32))),
        "key_proj": gaussian(seeds[1], (TOKENS, CH), 1.0, 6.0, ((0, 16), (1, 32))),
        "value_proj": gaussian(seeds[2], (TOKENS, CH), 1.0, 6.0, ((0, 16), (1, 32))),
        "filter_in": jnp.clip(jax.random.uniform(seeds[3], (POS, ORDER), jnp.float32, -16.0, 16.0), -16.0, 16.0),
        "filter_bias": jnp.clip(jax.random.uniform(seeds[4], (ORDER,), jnp.float32, -3.140625, 3.140625), -3.140625, 3.140625),
        "filter_out": gaussian(seeds[5], (ORDER, CH), ORDER ** -0.5, 0.75, ((1, 32),), jnp.float32),
        "decay_level": jnp.clip(1.0 * jax.random.uniform(seeds[6], (CH,), jnp.float32) ** block_levels(seeds[6], (CH,), ((0, 32),), -0.2, 0.2), 0.0, 1.0),
        "skip_gain": gaussian(seeds[7], (CH,), 1.0, 4.0, ((0, 32),), jnp.float32),
        "out_weight": bell_draw_with(seeds[8], (DOUT, CH), CH ** -0.5, 0.1875, ((1, 32),), (1, 0, 32, 2.75)),
    }


full_turn = 2.0 * math.pi

def generate(filter_in, filter_bias, filter_out, decay_level, length):
    half_count = POS // 2
    steps_int = jnp.arange(length, dtype=jnp.int32)
    frequency = jnp.arange(1, half_count + 1, dtype=jnp.int32)
    phases = (steps_int[:, None] * frequency[None, :] % length).astype(jnp.float32) * (full_turn / length)
    features = jnp.concatenate([jnp.sin(phases), jnp.cos(phases)], axis=1)
    hidden = jnp.sin(jnp.dot(features, filter_in, precision=lax.Precision.HIGHEST) + filter_bias)
    raw_values = jnp.dot(hidden, filter_out, precision=lax.Precision.HIGHEST)
    levels = jnp.maximum(2.0 * decay_level - 1.0, 0.0)
    decay_rate = 0.5 / length * jnp.exp(levels * math.log(length / 16.0))
    positions = steps_int.astype(jnp.float32)
    return raw_values * jnp.exp(-decay_rate[None, :] * positions[:, None])

def reference(query_proj, key_proj, value_proj, filter_in, filter_bias, filter_out, decay_level, skip_gain, out_weight):
    length = TOK_DEV * N_SEQ
    raw_taps = generate(filter_in, filter_bias, filter_out, decay_level, length)
    filter_taps = raw_taps / jnp.sqrt(lax.optimization_barrier(jnp.sum(raw_taps * raw_taps, axis=0)) + 1e-05)
    mixed_in = key_proj.astype(jnp.float32) * value_proj.astype(jnp.float32)
    spec_in = jnp.fft.rfft(mixed_in, n=2 * length, axis=0)
    spec_taps = jnp.fft.rfft(filter_taps, n=2 * length, axis=0)
    convolved = jnp.fft.irfft(spec_in * spec_taps, n=2 * length, axis=0)[:length]
    gated_rows = (query_proj.astype(jnp.float32) * (convolved + skip_gain[None, :] * mixed_in)).astype(jnp.bfloat16)
    slabs_in = gated_rows.reshape(length, N_CHAN, CH_DEV).transpose(1, 0, 2)
    slabs_weight = out_weight.reshape(DOUT, N_CHAN, CH_DEV).transpose(1, 0, 2)

    def accumulate(running_sum, slab_pair):
        partial_sum = jnp.dot(slab_pair[0], slab_pair[1].T, preferred_element_type=jnp.float32)
        rounded = lax.optimization_barrier(partial_sum.astype(jnp.bfloat16))
        return (running_sum + rounded.astype(jnp.float32), None)
    running_sum, unused = lax.scan(accumulate, jnp.zeros((length, DOUT), jnp.float32), (slabs_in, slabs_weight))
    return running_sum.astype(jnp.bfloat16)
```

```python
import functools
import math

import jax
import jax.numpy as jnp
from jax import lax
from jax.experimental import pallas as pl
from jax.experimental.pallas import tpu as pltpu
from jax.sharding import PartitionSpec as P

full_turn = 2.0 * math.pi
highest = lax.Precision.HIGHEST
f32 = jnp.float32
bf16 = jnp.bfloat16
vmem = pl.BlockSpec(memory_space=pltpu.VMEM)
smem = pl.BlockSpec(memory_space=pltpu.SMEM)
LANE = 128


def sine_of_turns(index, length):
    quarter = length // 4
    quadrant = (index + quarter // 2) // quarter
    rest = (index - quadrant * quarter).astype(f32) * (full_turn / length)
    sq = rest * rest
    sine = rest + rest * sq * (
        -1.6666667e-1 + sq * (8.3333333e-3 + sq * (-1.9841270e-4 + sq * 2.7557319e-6))
    )
    cosine = 1.0 + sq * (
        -0.5
        + sq * (4.1666667e-2 + sq * (-1.3888889e-3 + sq * (2.4801587e-5 - sq * 2.7557319e-7)))
    )
    quadrant = quadrant & 3
    odd = (quadrant & 1) == 1
    sin_sign = jnp.where(quadrant >= 2, -1.0, 1.0)
    cos_sign = jnp.where((quadrant == 1) | (quadrant == 2), -1.0, 1.0)
    return jnp.where(odd, cosine, sine) * sin_sign, jnp.where(odd, sine, cosine) * cos_sign


def sine(value):
    count = jnp.floor(value * (1.0 / math.pi) + 0.5)
    rest = value - count * 3.140625
    rest = rest - count * 9.67502593994140625e-4
    rest = rest - count * 1.509957990978376432e-7
    sq = rest * rest
    poly = -1.6666667e-1 + sq * (
        8.3333333e-3
        + sq
        * (-1.9841270e-4 + sq * (2.7557319e-6 + sq * (-2.5052108e-8 + sq * 1.6059044e-10)))
    )
    result = rest + rest * sq * poly
    odd = count - 2.0 * jnp.floor(count * 0.5)
    return result * (1.0 - 2.0 * odd)


def taps_kernel(length, place_ref, in_ref, bias_ref, out_ref, decay_ref, skip_ref, taps_ref, gain_ref, turned, columns):
    half = in_ref.shape[1] // 2
    share = taps_ref.shape[0]
    times = lax.broadcasted_iota(jnp.int32, (half, length), 1)
    freqs = lax.broadcasted_iota(jnp.int32, (half, length), 0) + 1
    sines, cosines = sine_of_turns((times * freqs) & (length - 1), length)
    features = jnp.concatenate([sines, cosines], axis=0)
    hidden = sine(
        jnp.dot(in_ref[...], features, precision=highest, preferred_element_type=f32)
        + bias_ref[...]
    )
    first = place_ref[0] * share
    turned[...] = out_ref[...].T
    columns[...] = jnp.concatenate(
        [
            jnp.broadcast_to(decay_ref[...], (LANE, decay_ref.shape[1])).T,
            jnp.broadcast_to(skip_ref[...], (LANE, skip_ref.shape[1])).T,
        ],
        axis=1,
    )
    rows = pl.ds(pl.multiple_of(first, share), share)
    raw = jnp.dot(turned[rows, :], hidden, precision=highest, preferred_element_type=f32)
    own = columns[rows, :]
    levels = jnp.maximum(2.0 * own[:, :1] - 1.0, 0.0)
    rate = (0.5 / length) * jnp.exp(levels * math.log(length / 16.0))
    position = lax.broadcasted_iota(jnp.int32, (share, length), 1).astype(f32)
    raw = raw * jnp.exp(-rate * position)
    energy = jnp.sum(raw * raw, axis=1, keepdims=True)
    taps_ref[...] = raw / jnp.sqrt(energy + 1e-05)
    gain_ref[...] = own[:, LANE:]


def prepare_kernel(query_ref, key_ref, value_ref, sent_ref):
    count, rows, width = sent_ref.shape
    share = rows // 2
    product = key_ref[...].astype(f32) * value_ref[...].astype(f32)
    sent_ref[:, :share, :] = product.T.reshape(count, share, width).astype(bf16)
    sent_ref[:, share:, :] = (
        query_ref[...].astype(f32).T.reshape(count, share, width).astype(bf16)
    )


def convolve_kernel(copies, got_ref, taps_ref, gain_ref, gated_ref, even, odd, signal, result):
    count, rows, width = got_ref.shape
    share = rows // 2
    zeros = jnp.zeros((count, LANE), f32)
    signal[...] = got_ref[:, :share, :].astype(f32)
    even[:count, :] = zeros
    odd[:count, :] = zeros
    lanes = lax.broadcasted_iota(jnp.int32, (LANE, LANE), 1)
    subs = lax.broadcasted_iota(jnp.int32, (LANE, LANE), 0)
    causal = lanes >= subs

    def turned(row):
        wide = jnp.broadcast_to(row, (LANE, LANE))
        return pltpu.roll(wide, 0, 1, stride=1, stride_axis=0)

    def channel(c, carry):
        even[count:, :] = signal[:, c, :LANE]
        odd[count:, :] = signal[:, c, LANE:]
        total = jnp.zeros((2 * count, LANE), f32)
        before = jnp.zeros((LANE, LANE), f32)
        for step in range(count):
            tiles = []
            for part in (0, 1):
                tile = 2 * step + part
                now = turned(taps_ref[c, tile * LANE : (tile + 1) * LANE].reshape(1, LANE))
                tiles.append(jnp.where(causal, now, before))
                before = now
            block = jnp.concatenate(tiles, axis=0).astype(bf16)
            even_now = even[count - step : 2 * count - step, :]
            odd_now = odd[count - step : 2 * count - step, :]
            odd_late = odd[count - step - 1 : 2 * count - step - 1, :]
            left = jnp.concatenate(
                [
                    jnp.concatenate([even_now, odd_late], axis=1),
                    jnp.concatenate([odd_now, even_now], axis=1),
                ],
                axis=0,
            ).astype(bf16)
            total = total + jnp.dot(left, block, preferred_element_type=f32)
        result[:, c, :LANE] = total[:count]
        result[:, c, LANE:] = total[count:]
        return carry

    for c in range(share):
        channel(c, 0)
    gain = jnp.concatenate([gain_ref[...], gain_ref[...]], axis=1)
    gated = got_ref[:, share:, :].astype(f32) * (
        result[...] + gain[None] * signal[...]
    )
    gated = gated.astype(bf16)
    for copy in range(copies):
        gated_ref[copy * count : (copy + 1) * count] = gated


def project_kernel(gated_ref, weight_ref, part_ref):
    parts, out_rows, depth = weight_ref.shape
    slots, width, own_rows = part_ref.shape
    gated = [gated_ref[k * depth : (k + 1) * depth, :].astype(f32).T.astype(bf16) for k in range(parts)]
    for slot in range(slots):
        total = jnp.zeros((width, own_rows), f32)
        for k in range(parts):
            total = total + lax.dot_general(
                gated[k],
                weight_ref[k, slot * own_rows : (slot + 1) * own_rows, :],
                (((1,), (1,)), ((), ())),
                preferred_element_type=f32,
            )
        part_ref[slot] = total.astype(bf16)


def body(
    query_proj,
    key_proj,
    value_proj,
    filter_in,
    filter_bias,
    filter_out,
    decay_level,
    skip_gain,
    out_weight,
):
    width, channels = key_proj.shape
    seqs = lax.axis_size("seq")
    chans = lax.axis_size("chan")
    cols = 4
    rows = chans // cols
    length = width * seqs
    share = channels // seqs
    order = filter_bias.shape[0]
    place = lax.axis_index("seq")
    col_groups = [[x * rows + y for x in range(cols)] for y in range(rows)]
    row_groups = [[x * rows + y for y in range(rows)] for x in range(cols)]
    back_groups = [
        [s * chans + x * rows + y for x in range(cols) for s in range(seqs)] for y in range(rows)
    ]

    weights = lax.all_to_all(
        out_weight.reshape(cols, out_weight.shape[0] // cols, channels),
        "chan",
        0,
        0,
        axis_index_groups=col_groups,
    )
    sent = pl.pallas_call(
        prepare_kernel,
        out_shape=jax.ShapeDtypeStruct((seqs, 2 * share, width), bf16),
        in_specs=[vmem] * 3,
        out_specs=vmem,
    )(query_proj, key_proj, value_proj)
    got = lax.all_to_all(sent, "seq", 0, 0)
    taps, gain = pl.pallas_call(
        functools.partial(taps_kernel, length),
        out_shape=(
            jax.ShapeDtypeStruct((share, length), f32),
            jax.ShapeDtypeStruct((share, LANE), f32),
        ),
        in_specs=[smem] + [vmem] * 5,
        out_specs=(vmem, vmem),
        scratch_shapes=[
            pltpu.VMEM((channels, order), f32),
            pltpu.VMEM((channels, 2 * LANE), f32),
        ],
    )(
        place.reshape(1),
        filter_in.T,
        filter_bias.reshape(order, 1),
        filter_out,
        decay_level.reshape(1, channels),
        skip_gain.reshape(1, channels),
    )
    gated = pl.pallas_call(
        functools.partial(convolve_kernel, cols),
        out_shape=jax.ShapeDtypeStruct((cols * seqs, share, width), bf16),
        in_specs=[vmem] * 3,
        out_specs=vmem,
        scratch_shapes=[
            pltpu.VMEM((2 * seqs, LANE), f32),
            pltpu.VMEM((2 * seqs, LANE), f32),
            pltpu.VMEM((seqs, share, width), f32),
            pltpu.VMEM((seqs, share, width), f32),
        ],
    )(got, taps, gain)
    gathered = lax.all_to_all(gated, ("seq", "chan"), 0, 0, axis_index_groups=back_groups)
    gathered = gathered.reshape(cols * channels, width)
    partial_sums = pl.pallas_call(
        project_kernel,
        out_shape=jax.ShapeDtypeStruct((rows, width, out_weight.shape[0] // chans), bf16),
        in_specs=[vmem] * 2,
        out_specs=vmem,
    )(gathered, weights)
    arrived = lax.all_to_all(partial_sums, "chan", 0, 0, axis_index_groups=row_groups)
    return arrived.astype(f32).sum(axis=0).astype(bf16)


def solution(mesh):
    placed = (
        P("seq", "chan"),
        P("seq", "chan"),
        P("seq", "chan"),
        P(),
        P(),
        P(None, "chan"),
        P("chan"),
        P("chan"),
        P(None, "chan"),
    )
    return jax.shard_map(
        body, mesh=mesh, in_specs=placed, out_specs=P("seq", "chan"), check_vma=False
    )
```
